32 devices in a mesh: row: 4 (over z), col: 8 (over y, x, core).
Axes of the slice: x: 2, y: 2, z: 4, core: 2. Of those that a mesh axis runs over, the one named last changes fastest.
Arguments:
- leaf_density: float32 [296, 262144], P(None, ('row', 'col')), may hold values from -6 to 6
- m2m: float32 [8, 296, 296], replicated, may hold values from -0.125 to 0.125
- v_source: int32 [512, 22], P(('row', 'col')), may hold values from 0 to 511, as said below
- v_class: int32 [512, 22], P(('row', 'col')), may hold values from 0 to 315
Outputs:
- coarse_density: float32 [296, 512], P(None, ('row', 'col'))
- far_field: float32 [296, 32768], P(None, ('row', 'col'))
The draws below stay inside these ranges and needn't reach their ends.
Inputs may be any that keep to these rules, and one draw needn't show every extreme that they name: Box b is held by the device that holds row b of v_source. For two different devices, the V-lists of one device's boxes name at most 2 distinct boxes of the other; those of each device name exactly 2 boxes of the next device in order.
All inputs are finite; a program needn't handle non-finite values.
Results may differ from the reference program's by a relative error of at most 0.0003.
Values sent between devices are 32-bit elements; how exact they have to be, the bound alone decides.
No kernel may reach another device: no remote copies, remote signals or barrier semaphores. Data moves between devices by JAX's collectives and lax.ppermute only.
A program may use at most 192 MiB of HBM per device.

```python
import math
import jax
import jax.numpy as jnp
import numpy as np
from jax import lax

S = 296
R = 64
VL = 22
CAP = 2
CLASSES = 316
PAR_DEV = 16
BOXES = 512
LEAVES = 4096


def draw_v_source(key, part):
    ndev = BOXES // PAR_DEV
    keys = jax.random.split(jax.random.fold_in(key, 7), 5)
    weight = jax.random.randint(keys[0], (ndev,), 0, 5)
    raw = jax.random.randint(keys[1], (ndev, ndev), 0, 60)
    counts = jnp.minimum(CAP, raw % (weight[None, :] + 1))
    target = jnp.arange(ndev)[:, None]
    source = jnp.arange(ndev)[None, :]
    distance = (source - target) % ndev
    counts = jnp.where(distance == 1, CAP, counts)
    counts = jnp.where(distance == 0, 0, counts)
    by_dist = counts[target, (target + source) % ndev]
    running = jnp.cumsum(by_dist, axis=1)
    kept = jnp.where(running <= VL * PAR_DEV - PAR_DEV, by_dist, 0)
    counts = kept[target, distance]
    perms = jax.vmap(lambda k: jax.random.permutation(k, PAR_DEV))(jax.random.split(keys[2], ndev * ndev))
    perms = perms.reshape(ndev, ndev, PAR_DEV)
    remote_ids = source[:, :, None] * PAR_DEV + perms[:, :, :CAP]
    remote_ok = jnp.arange(CAP)[None, None, :] < counts[:, :, None]
    local_ids = target * PAR_DEV + jnp.arange(PAR_DEV)[None, :]
    cand = jnp.concatenate([remote_ids.reshape(ndev, -1), local_ids], axis=1)
    usable = jnp.concatenate([remote_ok.reshape(ndev, -1), jnp.ones((ndev, PAR_DEV), bool)], axis=1)
    width_all = cand.shape[1]
    spot = jnp.cumsum(usable.astype(jnp.int32), axis=1) - 1
    total = jnp.sum(usable.astype(jnp.int32), axis=1)
    compact = jnp.zeros((ndev, width_all), jnp.int32)
    compact = compact.at[target, jnp.where(usable, spot, width_all)].set(cand.astype(jnp.int32), mode='drop')
    slots = PAR_DEV * VL
    picks = jax.random.randint(keys[3], (ndev, slots), 0, 1 << 20) % total[:, None]
    order = jnp.arange(slots)[None, :]
    chosen = jnp.where(order < total[:, None], order, picks)
    refs = jnp.take_along_axis(compact, chosen, axis=1)
    shuffle = jax.vmap(lambda k: jax.random.permutation(k, slots))(jax.random.split(keys[4], ndev))
    refs = jnp.take_along_axis(refs, shuffle, axis=1)
    return refs.reshape(ndev * PAR_DEV, VL).astype(jnp.int32)


def plant(drawn, key, smallest, top_value):
    index_at = [jax.random.randint(jax.random.fold_in(key, axis), (), 0, length) for axis, length in enumerate(drawn.shape)]
    main_axis = drawn.shape.index(max(drawn.shape))
    next_to = index_at[:main_axis] + [(index_at[main_axis] + 1) % drawn.shape[main_axis]] + index_at[main_axis + 1:]
    return drawn.at[tuple(index_at)].set(smallest).at[tuple(next_to)].set(top_value)


def block_scale(rng, dims, cuts, low, high):
    gain = 1.0
    for axis_at, blocks in cuts:
        steps = jax.random.uniform(jax.random.fold_in(jax.random.fold_in(rng, 6), axis_at), (blocks,), jnp.float32, low / len(cuts), high / len(cuts))
        gain = gain * jnp.repeat(jnp.exp(steps), dims[axis_at] // blocks).reshape((-1,) + (1,) * (len(dims) - 1 - axis_at))
    return gain


def centred(own_key, dims, scale, limit, cuts=(), kind=jnp.bfloat16):
    drawn = scale * jax.random.normal(own_key, dims, jnp.float32)
    if cuts:
        drawn = drawn * block_scale(own_key, dims, cuts, -0.22, 0.18)
    return jnp.clip(drawn, -limit, limit).astype(kind)


def setup_inputs(seed: int = 0) -> dict:
    seeds = jax.random.split(jax.random.key(seed), 5)
    return {
        "leaf_density": centred(seeds[0], (S, LEAVES * R), 1.0, 6.0, ((1, 32),), jnp.float32),
        "m2m": centred(seeds[1], (8, S, S), (8 * S) ** -0.5, 0.125, (), jnp.float32),
        "v_source": draw_v_source(jax.random.fold_in(seeds[4], 71), 0),
        "v_class": plant(jax.random.randint(seeds[3], (BOXES, VL), 0, CLASSES), jax.random.fold_in(seeds[3], 1), 0, CLASSES - 1).astype(jnp.int32),
    }


radius = 0.525
kernel_scale = 1.0 / (4.0 * math.pi)

def surface_points():
    edge_count = 2
    while edge_count ** 3 - (edge_count - 2) ** 3 != S:
        edge_count += 1
    coords = np.linspace(-1.0, 1.0, edge_count)
    lattice = np.stack(np.meshgrid(coords, coords, coords, indexing='ij'), -1).reshape(-1, 3)
    border = np.max(np.abs(lattice), axis=1) > 1.0 - 1e-09
    return lattice[border]

def offset_table():
    coords = np.arange(-3, 4)
    lattice = np.stack(np.meshgrid(coords, coords, coords, indexing='ij'), -1).reshape(-1, 3)
    farther = np.max(np.abs(lattice), axis=1) >= 2
    return lattice[farther]

def build_tiles(classes):
    highest = lax.Precision.HIGHEST
    table_arr = jnp.asarray(offset_table(), jnp.float32)
    one_hot = (classes[:, None] == jnp.arange(CLASSES, dtype=jnp.int32)[None, :]).astype(jnp.float32)
    offset = jnp.dot(one_hot, table_arr, precision=highest)
    points = jnp.asarray(surface_points() * radius, jnp.float32)
    dist_sq = jnp.zeros((classes.shape[0], S, S), jnp.float32)
    for comp in range(3):
        coord_pts = points[:, comp]
        delta = coord_pts[None, :, None] - offset[:, comp][:, None, None] - coord_pts[None, None, :]
        dist_sq = dist_sq + delta * delta
    return lax.rsqrt(dist_sq) * kernel_scale

def reference(leaf_density, m2m, v_source, v_class):
    highest = lax.Precision.HIGHEST
    box_total = v_source.shape[0]
    leaves = leaf_density.reshape(S, box_total, 8, R)
    box_dens = jnp.einsum('cij,jbcr->ibr', m2m, leaves, precision=highest)
    upper_dens = jnp.einsum('cij,jqcr->iqr', m2m, box_dens.reshape(S, box_total // 8, 8, R), precision=highest)
    coarse = jnp.einsum('cij,jucr->iur', m2m, upper_dens.reshape(S, box_total // 64, 8, R), precision=highest)
    coarse_density = coarse.reshape(S, -1)

    def one_box(pair):
        source_ids, classes = pair
        sources = jnp.take(box_dens, source_ids, axis=1)
        tile_set = build_tiles(classes)
        return jnp.einsum('kij,jkr->ir', tile_set, sources, precision=highest)
    result = lax.map(one_box, (v_source, v_class))
    far_field = jnp.transpose(result, (1, 0, 2)).reshape(S, -1)
    return (coarse_density, far_field)
```

```python
import functools
import math

import jax
import jax.numpy as jnp
import numpy as np
from jax import lax
from jax.experimental import pallas as pl
from jax.experimental.pallas import tpu as pltpu
from jax.sharding import PartitionSpec as P

CAP = 2
LANES = 128
KPAD = 384

radius = 0.525
kernel_scale = 1.0 / (4.0 * math.pi)
bf16 = jnp.bfloat16
f32 = jnp.float32


def surface_points(count):
    edge_count = 2
    while edge_count**3 - (edge_count - 2) ** 3 != count:
        edge_count += 1
    coords = np.linspace(-1.0, 1.0, edge_count)
    lattice = np.stack(np.meshgrid(coords, coords, coords, indexing="ij"), -1).reshape(-1, 3)
    border = np.max(np.abs(lattice), axis=1) > 1.0 - 1e-09
    return lattice[border]


def offset_table():
    coords = np.arange(-3, 4)
    lattice = np.stack(np.meshgrid(coords, coords, coords, indexing="ij"), -1).reshape(-1, 3)
    farther = np.max(np.abs(lattice), axis=1) >= 2
    return lattice[farther]


def low_lanes(rows):
    return lax.broadcasted_iota(jnp.int32, (rows, LANES), 1) < LANES // 2


def half_turn(value):
    return pltpu.roll(value, LANES // 2, 1)


def row_tiles(count):
    return [(start, min(16, count - start)) for start in range(0, count, 16)]


def split_store(value, rows, hi_ref, lo_ref, at_row, at_lane, lanes):
    hi = value.astype(bf16)
    lo = (value - hi.astype(f32)).astype(bf16)
    hi_ref[at_row : at_row + rows, at_lane : at_lane + lanes] = hi
    lo_ref[at_row : at_row + rows, at_lane : at_lane + lanes] = lo


def pair_columns(first, second, rows):
    low = low_lanes(rows)
    return (
        jnp.where(low, first, half_turn(second)),
        jnp.where(low, half_turn(first), second),
    )


def three_dots(m_hi, m_lo, x_hi, x_lo):
    out = jnp.dot(m_hi, x_hi, preferred_element_type=f32)
    out = out + jnp.dot(m_lo, x_hi, preferred_element_type=f32)
    return out + jnp.dot(m_hi, x_lo, preferred_element_type=f32)


def upward_kernel(leaf_ref, m_ref, out_ref, mh_ref, ml_ref, xh, xl):
    size = m_ref.shape[1]

    @pl.when(pl.program_id(0) == 0)
    def _():
        mh_ref[...] = jnp.zeros_like(mh_ref)
        ml_ref[...] = jnp.zeros_like(ml_ref)
        xh[...] = jnp.zeros_like(xh)
        xl[...] = jnp.zeros_like(xl)
        for child in range(8):
            for start, rows in row_tiles(size):
                split_store(
                    m_ref[child, start : start + rows, :], rows, mh_ref, ml_ref, start, child * KPAD, size
                )

    for slab in range(out_ref.shape[0]):
        for duo in range(4):
            left = slab * 8 * LANES + duo * LANES
            right = left + 4 * LANES
            for start, rows in row_tiles(size):
                even, odd = pair_columns(
                    leaf_ref[start : start + rows, left : left + LANES],
                    leaf_ref[start : start + rows, right : right + LANES],
                    rows,
                )
                split_store(even, rows, xh, xl, 2 * duo * KPAD + start, slab * LANES, LANES)
                split_store(odd, rows, xh, xl, (2 * duo + 1) * KPAD + start, slab * LANES, LANES)
    out = three_dots(mh_ref[...], ml_ref[...], xh[...], xl[...])
    for slab in range(out_ref.shape[0]):
        out_ref[slab] = out[:, slab * LANES : (slab + 1) * LANES]


def upward(leaf, m2m, slabs):
    size = m2m.shape[1]
    step = 2
    return pl.pallas_call(
        upward_kernel,
        grid=(slabs // step,),
        in_specs=[
            pl.BlockSpec((size, step * 8 * LANES), lambda i: (0, i)),
            pl.BlockSpec(m2m.shape, lambda i: (0, 0, 0)),
        ],
        out_specs=[
            pl.BlockSpec((step, size, LANES), lambda i: (i, 0, 0)),
            pl.BlockSpec((size, 8 * KPAD), lambda i: (0, 0)),
            pl.BlockSpec((size, 8 * KPAD), lambda i: (0, 0)),
        ],
        out_shape=[
            jax.ShapeDtypeStruct((slabs, size, LANES), f32),
            jax.ShapeDtypeStruct((size, 8 * KPAD), bf16),
            jax.ShapeDtypeStruct((size, 8 * KPAD), bf16),
        ],
        scratch_shapes=[
            pltpu.VMEM((8 * KPAD, step * LANES), bf16),
            pltpu.VMEM((8 * KPAD, step * LANES), bf16),
        ],
        cost_estimate=pl.CostEstimate(
            flops=2 * 8 * size * size * slabs * LANES * 3,
            bytes_accessed=4 * (leaf.size + m2m.size),
            transcendentals=0,
        ),
        name="upward",
    )(leaf, m2m)


def coarse_kernel(first_ref, pool_ref, mh_ref, ml_ref, out_ref, xh, xl, yh, yl):
    size = out_ref.shape[0]
    for ref in (xh, xl, yh, yl):
        ref[...] = jnp.zeros_like(ref)
    for duo in range(4):
        for start, rows in row_tiles(size):
            even, odd = pair_columns(
                pool_ref[duo, start : start + rows, :], pool_ref[4 + duo, start : start + rows, :], rows
            )
            split_store(even, rows, xh, xl, 2 * duo * KPAD + start, 0, LANES)
            split_store(odd, rows, xh, xl, (2 * duo + 1) * KPAD + start, 0, LANES)
    upper = three_dots(mh_ref[...], ml_ref[...], xh[...], xl[...])
    for start, rows in row_tiles(size):
        part = upper[start : start + rows]
        low = low_lanes(rows)
        split_store(jnp.where(low, part, 0.0), rows, yh, yl, start, 0, LANES)
        split_store(jnp.where(low, half_turn(part), 0.0), rows, yh, yl, KPAD + start, 0, LANES)
    at = pl.multiple_of(first_ref[0] * KPAD, LANES)
    out = three_dots(
        mh_ref[:, pl.ds(at, 2 * KPAD)], ml_ref[:, pl.ds(at, 2 * KPAD)], yh[...], yl[...]
    )
    out_ref[...] = out[:, : out_ref.shape[1]]


def coarse_partial(pool, mh, ml, first, rhs):
    slabs, size, _ = pool.shape
    vmem = pl.BlockSpec(memory_space=pltpu.VMEM)
    return pl.pallas_call(
        coarse_kernel,
        in_specs=[pl.BlockSpec(memory_space=pltpu.SMEM), vmem, vmem, vmem],
        out_specs=vmem,
        out_shape=jax.ShapeDtypeStruct((size, rhs), f32),
        scratch_shapes=[
            pltpu.VMEM((8 * KPAD, LANES), bf16),
            pltpu.VMEM((8 * KPAD, LANES), bf16),
            pltpu.VMEM((2 * KPAD, LANES), bf16),
            pltpu.VMEM((2 * KPAD, LANES), bf16),
        ],
        cost_estimate=pl.CostEstimate(
            flops=2 * 8 * size * size * 2 * LANES * 3,
            bytes_accessed=4 * pool.size + 4 * mh.size,
            transcendentals=0,
        ),
        name="coarse",
    )(first, pool, mh, ml)


def fold_rows(size):
    first = size // 2 // 16 * 16
    return first, size - first


def choose_kernel(count, slot, wanted_ref, pool_ref, out_ref, ready, sems):
    size = pool_ref.shape[1]
    upper, lower = fold_rows(size)

    def send(dest):
        return pltpu.make_async_copy(ready.at[dest], out_ref.at[dest], sems.at[dest])

    @pl.loop(0, count)
    def _(dest):
        box = wanted_ref[CAP * dest + slot]
        slab = lax.shift_right_logical(box, 1)
        odd = (box & 1) == 1
        for start, rows in row_tiles(lower):
            under = pool_ref[slab, upper + start : upper + start + rows, :]
            under = jnp.where(odd, under, half_turn(under))
            have = min(rows, upper - start)
            if have <= 0:
                over = jnp.zeros_like(under)
            else:
                over = pool_ref[slab, start : start + have, :]
                over = jnp.where(odd, half_turn(over), over)
                if have < rows:
                    over = jnp.concatenate([over, jnp.zeros((rows - have, LANES), f32)], axis=0)
            ready[dest, start : start + rows, :] = jnp.where(low_lanes(rows), over, under)
        send(dest).start()

    for dest in range(count):
        send(dest).wait()


def choose(pool, wanted, slot, after):
    dests = wanted.shape[0]
    size = pool.shape[1]
    shape = (dests, fold_rows(size)[1], LANES)
    return pl.pallas_call(
        functools.partial(choose_kernel, dests, slot),
        in_specs=[pl.BlockSpec(memory_space=pltpu.SMEM), pl.BlockSpec(memory_space=pltpu.VMEM)],
        out_specs=pl.BlockSpec(memory_space=pl.ANY),
        out_shape=jax.ShapeDtypeStruct(shape, f32),
        scratch_shapes=[pltpu.VMEM(shape, f32), pltpu.SemaphoreType.DMA((dests,))],
        cost_estimate=pl.CostEstimate(
            flops=0, bytes_accessed=4 * (pool.size + math.prod(shape)), transcendentals=0
        ),
        name="choose",
    )(tie(wanted.reshape(-1), after), pool)


def tie(value, after):
    return value if after is None else lax.optimization_barrier((value, after))[0]


MAIN = 256
TAIL = 64


def field_kernel(first, last, boxes, size, tbl_ref, list_ref, span_ref, col_ref, row_ref, pool_ref, *rest):
    rest = list(rest)
    acc_in = None if first else rest.pop(0)
    out_ref, sp, dist = rest[:3]
    rest = rest[3:]
    acc = rest.pop(0) if last else out_ref
    slabs, held, _ = pool_ref.shape
    upper, lower = fold_rows(size)
    folded = held != size
    rows_pad = dist.shape[0]
    if first:
        acc[...] = jnp.zeros_like(acc)
    else:
        carried = pltpu.make_async_copy(acc_in, acc, rest.pop(0))
        carried.start()

    for start, rows in row_tiles(rows_pad):
        for lane in range(0, KPAD, LANES):
            total = jnp.zeros((rows, LANES), f32)
            for comp in range(3):
                delta = (
                    col_ref[comp, start : start + rows, :] - row_ref[comp : comp + 1, lane : lane + LANES]
                )
                total = total + delta * delta
            dist[start : start + rows, lane : lane + LANES] = total

    @pl.loop(0, slabs)
    def _(slab):
        def keep(source, at, value):
            lesser = value - value.astype(bf16).astype(f32)
            sp[source, at : at + value.shape[0], :] = jnp.where(
                low_lanes(value.shape[0]), value, lesser
            ).astype(bf16)

        def empty(source, at):
            rows = MAIN + TAIL - at
            sp[source, at : at + rows, :] = jnp.zeros((rows, LANES), bf16)

        for start, rows in row_tiles(held):
            value = pool_ref[slab, start : start + rows, :]
            if rows < 16:
                value = jnp.concatenate([value, jnp.zeros((16 - rows, LANES), f32)], axis=0)
            low = low_lanes(16)
            turned = half_turn(value)
            left, right = jnp.where(low, value, turned), jnp.where(low, turned, value)
            if folded:
                if start < upper:
                    keep(slab, start, left)
                keep(slab, upper + start, right)
            else:
                keep(2 * slab, start, left)
                keep(2 * slab + 1, start, right)
        ending = -(-size // 16) * 16
        for source in (slab,) if folded else (2 * slab, 2 * slab + 1):
            empty(source, ending)

    if not first:
        carried.wait()
    begin = span_ref[0]
    count = span_ref[1]

    def read(index):
        code = list_ref[begin + jnp.minimum(index, count - 1)]
        cls = lax.shift_right_logical(code, 12)
        source = code & 255
        target = jnp.where(index < count, lax.shift_right_logical(code, 8) & 15, boxes)
        return [tbl_ref[cls * 3 + comp] for comp in range(3)], source, target

    def duo(index, sums):
        members = [read(index), read(index + 1)]
        shifts, twice = [], []
        for offset, _, _ in members:
            base = offset[0] * offset[0] + offset[1] * offset[1] + offset[2] * offset[2]
            double = [2.0 * comp for comp in offset]
            twice.append(double)
            shifts.append(
                double[0] * row_ref[0:1, :] + double[1] * row_ref[1:2, :] + double[2] * row_ref[2:3, :] + base
            )
        low = low_lanes(16)
        shift_tail = jnp.where(low[:1], shifts[0][:, MAIN:], shifts[1][:, MAIN:])
        tiles = []
        for start, rows in row_tiles(rows_pad):
            point = [col_ref[comp, start : start + rows, :] for comp in range(3)]
            owns = [d[0] * point[0] + d[1] * point[1] + d[2] * point[2] for d in twice]
            parts = []
            for own, shift in zip(owns, shifts):
                own = jnp.concatenate([own, own], axis=1)
                value = lax.rsqrt(dist[start : start + rows, :MAIN] + (shift[:, :MAIN] - own))
                hi = value.astype(bf16)
                parts += [hi, (value - hi.astype(f32)).astype(bf16)]
            own = jnp.where(low, owns[0], owns[1])
            value = lax.rsqrt(dist[start : start + rows, MAIN:] + (shift_tail - own))
            hi = value.astype(bf16)
            parts.append(jnp.concatenate([hi, (value - hi.astype(f32)).astype(bf16)], axis=1))
            tiles.append(parts)

        mains, tails = [], []
        for at, (_, source, _) in enumerate(members):
            for begin_row, rows, kept in ((0, MAIN, mains), (MAIN, TAIL, tails)):
                part = sp[source, begin_row : begin_row + rows, :]
                empty = jnp.zeros_like(part)
                kept.append(jnp.concatenate([part, empty] if at == 0 else [empty, part], axis=1))
        stationary = [mains[0], mains[0], mains[1], mains[1], jnp.concatenate(tails * 2, axis=0)]
        for chunk, rhs in enumerate(stationary):
            fresh = chunk not in (1, 3)
            for unit in range(2):
                if fresh:
                    pltpu.matmul_push_rhs(rhs, 0, unit)
                for at in range(unit, len(tiles), 2):
                    pltpu.matmul_acc_lhs(sums[at], tiles[at][chunk], 0 if at == unit and fresh else None)
        for at, (start, rows) in enumerate(row_tiles(rows_pad)):
            have = min(rows, size - start)
            product = pltpu.matmul_pop(sums[at])
            for number, (_, _, target) in enumerate(members):
                mine = product[:have, number * LANES : (number + 1) * LANES]
                acc[target, start : start + have, :] = acc[target, start : start + have, :] + mine

    def duos(*flat):
        sums = flat[: len(flat) // 2], flat[len(flat) // 2 :]

        whole = lax.shift_right_logical(count, 3)

        @pl.loop(0, whole)
        def _(step):
            for half in range(4):
                duo(8 * step + 2 * half, sums[half % 2])

        @pl.loop(4 * whole, lax.shift_right_logical(count + 1, 1))
        def _(step):
            duo(2 * step, sums[0])

    tiles_of = enumerate(row_tiles(rows_pad))
    kinds = [pltpu.ACC(at % 2)((rows, 256), f32) for at, (_, rows) in tiles_of]
    pl.run_scoped(duos, *kinds, *kinds)

    if last:
        for slab in range(boxes // 2):
            for start, rows in row_tiles(size):
                left = acc[2 * slab, start : start + rows, :]
                right = acc[2 * slab + 1, start : start + rows, :]
                out_ref[start : start + rows, slab * LANES : (slab + 1) * LANES] = kernel_scale * jnp.where(
                    low_lanes(rows), left + half_turn(left), right + half_turn(right)
                )


def field(pool, acc, listing, span, boxes, size, last, after):
    slabs, held, _ = pool.shape
    sources = slabs if held != size else 2 * slabs
    points = surface_points(size) * radius
    rows_pad = -(-size // 16) * 16
    col = np.zeros((3, rows_pad, LANES), np.float32)
    col[:, :size] = points.T[:, :, None]
    row = np.zeros((8, KPAD), np.float32)
    row[:3, :size] = points.T
    row[:, MAIN + TAIL :] = row[:, MAIN : MAIN + TAIL]
    vmem = pl.BlockSpec(memory_space=pltpu.VMEM)
    smem = pl.BlockSpec(memory_space=pltpu.SMEM)
    first = acc is None
    args = [jnp.asarray(offset_table().reshape(-1), f32), listing, tie(span, after), jnp.asarray(col), jnp.asarray(row), pool]
    specs = [smem, smem, smem, vmem, vmem, vmem]
    sums = (boxes + 1, size, LANES)
    scratch = [
        pltpu.VMEM((sources, MAIN + TAIL, LANES), bf16),
        pltpu.VMEM((rows_pad, KPAD), f32),
    ]
    if last:
        scratch.append(pltpu.VMEM(sums, f32))
    if not first:
        args.append(acc)
        specs.append(pl.BlockSpec(memory_space=pl.ANY))
        scratch.append(pltpu.SemaphoreType.DMA)
    pairs = listing.shape[0] // 3
    return pl.pallas_call(
        functools.partial(field_kernel, first, last, boxes, size),
        in_specs=specs,
        out_specs=vmem,
        out_shape=jax.ShapeDtypeStruct((size, boxes * LANES // 2) if last else sums, f32),
        scratch_shapes=scratch,
        compiler_params=pltpu.CompilerParams(vmem_limit_bytes=60 * 1024 * 1024),
        cost_estimate=pl.CostEstimate(
            flops=2 * rows_pad * 2 * KPAD * LANES * pairs,
            bytes_accessed=4 * pool.size,
            transcendentals=rows_pad * KPAD * pairs,
        ),
        name="field",
    )(*args)


def stage_lists(stage, codes, stages):
    slots = codes.shape[0]
    order = jnp.arange(slots, dtype=jnp.int32)
    ahead = (stage[None, :] < stage[:, None]) | (
        (stage[None, :] == stage[:, None]) & (order[None, :] < order[:, None])
    )
    place = jnp.sum(ahead.astype(jnp.int32), axis=1)
    listing = jnp.sum(jnp.where(place[None, :] == order[:, None], codes[None, :], 0), axis=1)
    numbers = jnp.arange(stages, dtype=jnp.int32)
    counts = jnp.sum((stage[None, :] == numbers[:, None]).astype(jnp.int32), axis=1)
    begins = jnp.sum((stage[None, :] < numbers[:, None]).astype(jnp.int32), axis=1)
    return listing, jnp.stack([begins, counts], axis=1)


def body(leaf_density, m2m, v_source, v_class):
    axes = ("row", "col")
    size = m2m.shape[1]
    box_count = v_source.shape[0]
    rhs = leaf_density.shape[1] // (8 * box_count)
    device, ndev = lax.axis_index(axes), lax.axis_size(axes)

    ids = v_source.reshape(-1)
    owner = ids // box_count
    named = ids[:, None] == jnp.arange(ndev * box_count, dtype=jnp.int32)[None, :]
    needed = jnp.any(named, axis=0).reshape(ndev, box_count)
    local = jnp.arange(box_count, dtype=jnp.int32)
    earlier = (local[None, :] < local[:, None])[None]
    rank = jnp.sum((needed[:, None, :] & earlier).astype(jnp.int32), axis=2)
    slots = jnp.arange(CAP, dtype=jnp.int32)
    hit = needed[:, None, :] & (rank[:, None, :] == slots[None, :, None])
    wanted = jnp.sum(jnp.where(hit, local[None, None, :], 0), axis=2)

    def exchange(value):
        return lax.all_to_all(value, axes, split_axis=0, concat_axis=0, tiled=True)

    requested = exchange(wanted)
    pool, mh, ml = upward(leaf_density, m2m, box_count // 2)
    chosen = choose(pool, requested, 0, None)
    received = exchange(chosen)

    pair_rank = jnp.sum(jnp.where(named, rank.reshape(-1)[None, :], 0), axis=1)
    mine = owner == device
    source = jnp.where(mine, ids % box_count, owner)
    target = jnp.repeat(jnp.arange(box_count, dtype=jnp.int32), v_source.shape[1])
    codes = v_class.reshape(-1) * 4096 + target * 256 + source
    listing, spans = stage_lists(jnp.where(mine, 0, 1 + pair_rank), codes, 1 + CAP)

    first = (device * (box_count // 8)) % 8
    current = coarse_partial(pool, mh, ml, tie(first.reshape(1).astype(jnp.int32), chosen), rhs)
    group_size = 64 // box_count
    for bit in range(group_size.bit_length() - 1):
        pairs = [(i, i ^ (1 << bit)) for i in range(ndev)]
        current = current + lax.ppermute(current, axes, pairs)
    share = rhs // group_size
    coarse = lax.dynamic_slice_in_dim(current, (device % group_size) * share, share, 1)

    chosen_second = choose(pool, requested, 1, chosen)
    acc = field(pool, None, listing, spans[0], box_count, size, False, chosen_second)
    received_second = exchange(tie(chosen_second, (received, acc, coarse)))
    acc = field(received, acc, listing, spans[1], box_count, size, False, None)
    out = field(received_second, acc, listing, spans[2], box_count, size, True, None)
    return (coarse, out)


def solution(mesh):
    both = ("row", "col")
    return jax.shard_map(
        body,
        mesh=mesh,
        in_specs=(P(None, both), P(), P(both, None), P(both, None)),
        out_specs=(P(None, both), P(None, both)),
        check_vma=False,
    )
```

```python
import functools
import math

import jax
import jax.numpy as jnp
import numpy as np
from jax import lax
from jax.experimental import pallas as pl
from jax.experimental.pallas import tpu as pltpu
from jax.sharding import PartitionSpec as P

CAP = 2
LANES = 128
KPAD = 384

radius = 0.525
kernel_scale = 1.0 / (4.0 * math.pi)
bf16 = jnp.bfloat16
f32 = jnp.float32


def surface_points(count):
    edge_count = 2
    while edge_count**3 - (edge_count - 2) ** 3 != count:
        edge_count += 1
    coords = np.linspace(-1.0, 1.0, edge_count)
    lattice = np.stack(np.meshgrid(coords, coords, coords, indexing="ij"), -1).reshape(-1, 3)
    border = np.max(np.abs(lattice), axis=1) > 1.0 - 1e-09
    return lattice[border]


def offset_table():
    coords = np.arange(-3, 4)
    lattice = np.stack(np.meshgrid(coords, coords, coords, indexing="ij"), -1).reshape(-1, 3)
    farther = np.max(np.abs(lattice), axis=1) >= 2
    return lattice[farther]


def low_lanes(rows):
    return lax.broadcasted_iota(jnp.int32, (rows, LANES), 1) < LANES // 2


def half_turn(value):
    return pltpu.roll(value, LANES // 2, 1)


def row_tiles(count):
    return [(start, min(16, count - start)) for start in range(0, count, 16)]


def split_store(value, rows, hi_ref, lo_ref, at_row, at_lane, lanes):
    hi = value.astype(bf16)
    lo = (value - hi.astype(f32)).astype(bf16)
    hi_ref[at_row : at_row + rows, at_lane : at_lane + lanes] = hi
    lo_ref[at_row : at_row + rows, at_lane : at_lane + lanes] = lo


def pair_columns(first, second, rows):
    low = low_lanes(rows)
    return (
        jnp.where(low, first, half_turn(second)),
        jnp.where(low, half_turn(first), second),
    )


def three_dots(m_hi, m_lo, x_hi, x_lo):
    out = jnp.dot(m_hi, x_hi, preferred_element_type=f32)
    out = out + jnp.dot(m_lo, x_hi, preferred_element_type=f32)
    return out + jnp.dot(m_hi, x_lo, preferred_element_type=f32)


def upward_kernel(leaf_ref, m_ref, out_ref, mh_ref, ml_ref, xh, xl):
    size = m_ref.shape[1]

    @pl.when(pl.program_id(0) == 0)
    def _():
        mh_ref[...] = jnp.zeros_like(mh_ref)
        ml_ref[...] = jnp.zeros_like(ml_ref)
        xh[...] = jnp.zeros_like(xh)
        xl[...] = jnp.zeros_like(xl)
        for child in range(8):
            for start, rows in row_tiles(size):
                split_store(
                    m_ref[child, start : start + rows, :], rows, mh_ref, ml_ref, start, child * KPAD, size
                )

    for slab in range(out_ref.shape[0]):
        for duo in range(4):
            left = slab * 8 * LANES + duo * LANES
            right = left + 4 * LANES
            for start, rows in row_tiles(size):
                even, odd = pair_columns(
                    leaf_ref[start : start + rows, left : left + LANES],
                    leaf_ref[start : start + rows, right : right + LANES],
                    rows,
                )
                split_store(even, rows, xh, xl, 2 * duo * KPAD + start, slab * LANES, LANES)
                split_store(odd, rows, xh, xl, (2 * duo + 1) * KPAD + start, slab * LANES, LANES)
    out = three_dots(mh_ref[...], ml_ref[...], xh[...], xl[...])
    for slab in range(out_ref.shape[0]):
        out_ref[slab] = out[:, slab * LANES : (slab + 1) * LANES]


def upward(leaf, m2m, slabs):
    size = m2m.shape[1]
    step = 2
    return pl.pallas_call(
        upward_kernel,
        grid=(slabs // step,),
        in_specs=[
            pl.BlockSpec((size, step * 8 * LANES), lambda i: (0, i)),
            pl.BlockSpec(m2m.shape, lambda i: (0, 0, 0)),
        ],
        out_specs=[
            pl.BlockSpec((step, size, LANES), lambda i: (i, 0, 0)),
            pl.BlockSpec((size, 8 * KPAD), lambda i: (0, 0)),
            pl.BlockSpec((size, 8 * KPAD), lambda i: (0, 0)),
        ],
        out_shape=[
            jax.ShapeDtypeStruct((slabs, size, LANES), f32),
            jax.ShapeDtypeStruct((size, 8 * KPAD), bf16),
            jax.ShapeDtypeStruct((size, 8 * KPAD), bf16),
        ],
        scratch_shapes=[
            pltpu.VMEM((8 * KPAD, step * LANES), bf16),
            pltpu.VMEM((8 * KPAD, step * LANES), bf16),
        ],
        cost_estimate=pl.CostEstimate(
            flops=2 * 8 * size * size * slabs * LANES * 3,
            bytes_accessed=4 * (leaf.size + m2m.size),
            transcendentals=0,
        ),
        name="upward",
    )(leaf, m2m)


def coarse_kernel(first_ref, pool_ref, mh_ref, ml_ref, out_ref, xh, xl, yh, yl):
    size = out_ref.shape[0]
    for ref in (xh, xl, yh, yl):
        ref[...] = jnp.zeros_like(ref)
    for duo in range(4):
        for start, rows in row_tiles(size):
            even, odd = pair_columns(
                pool_ref[duo, start : start + rows, :], pool_ref[4 + duo, start : start + rows, :], rows
            )
            split_store(even, rows, xh, xl, 2 * duo * KPAD + start, 0, LANES)
            split_store(odd, rows, xh, xl, (2 * duo + 1) * KPAD + start, 0, LANES)
    upper = three_dots(mh_ref[...], ml_ref[...], xh[...], xl[...])
    for start, rows in row_tiles(size):
        part = upper[start : start + rows]
        low = low_lanes(rows)
        split_store(jnp.where(low, part, 0.0), rows, yh, yl, start, 0, LANES)
        split_store(jnp.where(low, half_turn(part), 0.0), rows, yh, yl, KPAD + start, 0, LANES)
    at = pl.multiple_of(first_ref[0] * KPAD, LANES)
    out = three_dots(
        mh_ref[:, pl.ds(at, 2 * KPAD)], ml_ref[:, pl.ds(at, 2 * KPAD)], yh[...], yl[...]
    )
    out_ref[...] = out[:, : out_ref.shape[1]]


def coarse_partial(pool, mh, ml, first, rhs):
    slabs, size, _ = pool.shape
    vmem = pl.BlockSpec(memory_space=pltpu.VMEM)
    return pl.pallas_call(
        coarse_kernel,
        in_specs=[pl.BlockSpec(memory_space=pltpu.SMEM), vmem, vmem, vmem],
        out_specs=vmem,
        out_shape=jax.ShapeDtypeStruct((size, rhs), f32),
        scratch_shapes=[
            pltpu.VMEM((8 * KPAD, LANES), bf16),
            pltpu.VMEM((8 * KPAD, LANES), bf16),
            pltpu.VMEM((2 * KPAD, LANES), bf16),
            pltpu.VMEM((2 * KPAD, LANES), bf16),
        ],
        cost_estimate=pl.CostEstimate(
            flops=2 * 8 * size * size * 2 * LANES * 3,
            bytes_accessed=4 * pool.size + 4 * mh.size,
            transcendentals=0,
        ),
        name="coarse",
    )(first, pool, mh, ml)


def fold_rows(size):
    first = size // 2 // 16 * 16
    return first, size - first


def choose_kernel(count, slot, wanted_ref, pool_ref, out_ref, ready, sems):
    size = pool_ref.shape[1]
    upper, lower = fold_rows(size)

    def send(dest):
        return pltpu.make_async_copy(ready.at[dest], out_ref.at[dest], sems.at[dest])

    @pl.loop(0, count, unroll=4)
    def _(dest):
        box = wanted_ref[dest, slot]
        slab = lax.shift_right_logical(box, 1)
        odd = (box & 1) == 1
        for start, rows in row_tiles(lower):
            under = pool_ref[slab, upper + start : upper + start + rows, :]
            have = min(rows, upper - start)
            if have <= 0:
                over = jnp.zeros_like(under)
            else:
                over = pool_ref[slab, start : start + have, :]
                if have < rows:
                    over = jnp.concatenate([over, jnp.zeros((rows - have, LANES), f32)], axis=0)
            turned = half_turn(jnp.where(odd, over, under))
            low = low_lanes(rows)
            ready[dest, start : start + rows, :] = jnp.where(
                odd, jnp.where(low, turned, under), jnp.where(low, over, turned)
            )
        send(dest).start()

    for dest in range(count):
        send(dest).wait()


def choose(pool, wanted, slot, after):
    dests = wanted.shape[0]
    size = pool.shape[1]
    shape = (dests, fold_rows(size)[1], LANES)
    return pl.pallas_call(
        functools.partial(choose_kernel, dests, slot),
        in_specs=[pl.BlockSpec(memory_space=pltpu.SMEM), pl.BlockSpec(memory_space=pltpu.VMEM)],
        out_specs=pl.BlockSpec(memory_space=pl.ANY),
        out_shape=jax.ShapeDtypeStruct(shape, f32),
        scratch_shapes=[pltpu.VMEM(shape, f32), pltpu.SemaphoreType.DMA((dests,))],
        cost_estimate=pl.CostEstimate(
            flops=0, bytes_accessed=4 * (pool.size + math.prod(shape)), transcendentals=0
        ),
        name="choose",
    )(tie(wanted, after), pool)


def tie(value, after):
    return value if after is None else lax.optimization_barrier((value, after))[0]


MAIN = 256
TAIL = 64


def field_kernel(first, last, boxes, size, tbl_ref, list_ref, span_ref, col_ref, row_ref, pool_hbm, *rest):
    rest = list(rest)
    acc_hbm = None if first else rest.pop(0)
    out_ref, acc, pool_ref, sp, dist, arrived, carried = rest
    slabs, held, _ = pool_ref.shape
    upper, lower = fold_rows(size)
    folded = held != size
    rows_pad = dist.shape[0]

    def fetch(slab):
        return pltpu.make_async_copy(pool_hbm.at[slab], pool_ref.at[slab], arrived.at[slab])

    for slab in range(slabs):
        fetch(slab).start()
    if first:
        acc[...] = jnp.zeros_like(acc)
    else:
        acc_copy = pltpu.make_async_copy(acc_hbm, acc, carried)
        acc_copy.start()

    for start, rows in row_tiles(rows_pad):
        for lane in range(0, KPAD, LANES):
            total = jnp.zeros((rows, LANES), f32)
            for comp in range(3):
                delta = (
                    col_ref[comp, start : start + rows, :] - row_ref[comp : comp + 1, lane : lane + LANES]
                )
                total = total + delta * delta
            dist[start : start + rows, lane : lane + LANES] = total

    @pl.loop(0, slabs)
    def _(slab):
        fetch(slab).wait()

        def keep(source, at, value):
            lesser = value - value.astype(bf16).astype(f32)
            sp[source, at : at + value.shape[0], :] = jnp.where(
                low_lanes(value.shape[0]), value, lesser
            ).astype(bf16)

        def empty(source, at):
            rows = MAIN + TAIL - at
            sp[source, at : at + rows, :] = jnp.zeros((rows, LANES), bf16)

        for start, rows in row_tiles(held):
            value = pool_ref[slab, start : start + rows, :]
            if rows < 16:
                value = jnp.concatenate([value, jnp.zeros((16 - rows, LANES), f32)], axis=0)
            low = low_lanes(16)
            turned = half_turn(value)
            left, right = jnp.where(low, value, turned), jnp.where(low, turned, value)
            if folded:
                if start < upper:
                    keep(slab, start, left)
                keep(slab, upper + start, right)
            else:
                keep(2 * slab, start, left)
                keep(2 * slab + 1, start, right)
        ending = -(-size // 16) * 16
        for source in (slab,) if folded else (2 * slab, 2 * slab + 1):
            empty(source, ending)

    if not first:
        acc_copy.wait()
    begin = span_ref[0]
    count = span_ref[1]

    def read(index):
        code = list_ref[begin + jnp.minimum(index, count - 1)]
        cls = lax.shift_right_logical(code, 12)
        source = code & 255
        target = jnp.where(index < count, lax.shift_right_logical(code, 8) & 15, boxes)
        return [tbl_ref[cls * 3 + comp] for comp in range(3)], source, target

    def duo(index, sums):
        members = [read(index), read(index + 1)]
        shifts, twice = [], []
        for offset, _, _ in members:
            base = offset[0] * offset[0] + offset[1] * offset[1] + offset[2] * offset[2]
            double = [2.0 * comp for comp in offset]
            twice.append(double)
            shifts.append(
                double[0] * row_ref[0:1, :] + double[1] * row_ref[1:2, :] + double[2] * row_ref[2:3, :] + base
            )
        low = low_lanes(16)
        shift_tail = jnp.where(low[:1], shifts[0][:, MAIN:], shifts[1][:, MAIN:])
        tiles = []
        for start, rows in row_tiles(rows_pad):
            point = [col_ref[comp, start : start + rows, :] for comp in range(3)]
            owns = [d[0] * point[0] + d[1] * point[1] + d[2] * point[2] for d in twice]
            parts = []
            for own, shift in zip(owns, shifts):
                own = jnp.concatenate([own, own], axis=1)
                value = lax.rsqrt(dist[start : start + rows, :MAIN] + (shift[:, :MAIN] - own))
                hi = value.astype(bf16)
                parts += [hi, (value - hi.astype(f32)).astype(bf16)]
            own = jnp.where(low, owns[0], owns[1])
            value = lax.rsqrt(dist[start : start + rows, MAIN:] + (shift_tail - own))
            hi = value.astype(bf16)
            parts.append(jnp.concatenate([hi, (value - hi.astype(f32)).astype(bf16)], axis=1))
            tiles.append(parts)

        mains, tails = [], []
        for at, (_, source, _) in enumerate(members):
            for begin_row, rows, kept in ((0, MAIN, mains), (MAIN, TAIL, tails)):
                part = sp[source, begin_row : begin_row + rows, :]
                empty = jnp.zeros_like(part)
                kept.append(jnp.concatenate([part, empty] if at == 0 else [empty, part], axis=1))
        stationary = [mains[0], mains[0], mains[1], mains[1], jnp.concatenate(tails * 2, axis=0)]
        for chunk, rhs in enumerate(stationary):
            fresh = chunk not in (1, 3)
            for unit in range(2):
                if fresh:
                    pltpu.matmul_push_rhs(rhs, 0, unit)
                for at in range(unit, len(tiles), 2):
                    pltpu.matmul_acc_lhs(sums[at], tiles[at][chunk], 0 if at == unit and fresh else None)
        for at, (start, rows) in enumerate(row_tiles(rows_pad)):
            have = min(rows, size - start)
            product = pltpu.matmul_pop(sums[at])
            for number, (_, _, target) in enumerate(members):
                mine = product[:have, number * LANES : (number + 1) * LANES]
                acc[target, start : start + have, :] = acc[target, start : start + have, :] + mine

    def duos(*flat):
        sums = flat[: len(flat) // 2], flat[len(flat) // 2 :]

        whole = lax.shift_right_logical(count, 3)

        @pl.loop(0, whole)
        def _(step):
            for half in range(4):
                duo(8 * step + 2 * half, sums[half % 2])

        @pl.loop(4 * whole, lax.shift_right_logical(count + 1, 1))
        def _(step):
            duo(2 * step, sums[0])

    tiles_of = enumerate(row_tiles(rows_pad))
    kinds = [pltpu.ACC(at % 2)((rows, 256), f32) for at, (_, rows) in tiles_of]
    pl.run_scoped(duos, *kinds, *kinds)

    if not last:
        result = pltpu.make_async_copy(acc, out_ref, carried)
        result.start()
        result.wait()
    else:
        for slab in range(boxes // 2):
            for start, rows in row_tiles(size):
                left = acc[2 * slab, start : start + rows, :]
                right = acc[2 * slab + 1, start : start + rows, :]
                out_ref[start : start + rows, slab * LANES : (slab + 1) * LANES] = kernel_scale * jnp.where(
                    low_lanes(rows), left + half_turn(left), right + half_turn(right)
                )


def field(pool, acc, listing, span, boxes, size, last, after):
    slabs, held, _ = pool.shape
    sources = slabs if held != size else 2 * slabs
    points = surface_points(size) * radius
    rows_pad = -(-size // 16) * 16
    col = np.zeros((3, rows_pad, LANES), np.float32)
    col[:, :size] = points.T[:, :, None]
    row = np.zeros((8, KPAD), np.float32)
    row[:3, :size] = points.T
    row[:, MAIN + TAIL :] = row[:, MAIN : MAIN + TAIL]
    vmem = pl.BlockSpec(memory_space=pltpu.VMEM)
    smem = pl.BlockSpec(memory_space=pltpu.SMEM)
    first = acc is None
    args = [jnp.asarray(offset_table().reshape(-1), f32), listing, tie(span, after), jnp.asarray(col), jnp.asarray(row), pool]
    hbm = pl.BlockSpec(memory_space=pltpu.HBM)
    specs = [smem, smem, smem, vmem, vmem, hbm]
    sums = (boxes + 1, size, LANES)
    scratch = [
        pltpu.VMEM(sums, f32),
        pltpu.VMEM(pool.shape, f32),
        pltpu.VMEM((sources, MAIN + TAIL, LANES), bf16),
        pltpu.VMEM((rows_pad, KPAD), f32),
        pltpu.SemaphoreType.DMA((slabs,)),
        pltpu.SemaphoreType.DMA,
    ]
    if not first:
        args.append(acc)
        specs.append(hbm)
    pairs = listing.shape[0] // 3
    return pl.pallas_call(
        functools.partial(field_kernel, first, last, boxes, size),
        in_specs=specs,
        out_specs=vmem if last else hbm,
        out_shape=jax.ShapeDtypeStruct((size, boxes * LANES // 2) if last else sums, f32),
        scratch_shapes=scratch,
        compiler_params=pltpu.CompilerParams(vmem_limit_bytes=60 * 1024 * 1024),
        cost_estimate=pl.CostEstimate(
            flops=2 * rows_pad * 2 * KPAD * LANES * pairs,
            bytes_accessed=4 * pool.size,
            transcendentals=rows_pad * KPAD * pairs,
        ),
        name="field",
    )(*args)


def stage_lists(stage, codes, stages):
    slots = codes.shape[0]
    order = jnp.arange(slots, dtype=jnp.int32)
    ahead = (stage[None, :] < stage[:, None]) | (
        (stage[None, :] == stage[:, None]) & (order[None, :] < order[:, None])
    )
    place = jnp.sum(ahead.astype(jnp.int32), axis=1)
    listing = jnp.sum(jnp.where(place[None, :] == order[:, None], codes[None, :], 0), axis=1)
    numbers = jnp.arange(stages, dtype=jnp.int32)
    counts = jnp.sum((stage[None, :] == numbers[:, None]).astype(jnp.int32), axis=1)
    begins = jnp.sum((stage[None, :] < numbers[:, None]).astype(jnp.int32), axis=1)
    return listing, jnp.stack([begins, counts], axis=1)


def body(leaf_density, m2m, v_source, v_class):
    axes = ("row", "col")
    size = m2m.shape[1]
    box_count = v_source.shape[0]
    rhs = leaf_density.shape[1] // (8 * box_count)
    device, ndev = lax.axis_index(axes), lax.axis_size(axes)

    ids = v_source.reshape(-1)
    owner = ids // box_count
    named = ids[:, None] == jnp.arange(ndev * box_count, dtype=jnp.int32)[None, :]
    needed = jnp.any(named, axis=0).reshape(ndev, box_count)
    local = jnp.arange(box_count, dtype=jnp.int32)
    earlier = (local[None, :] < local[:, None])[None]
    rank = jnp.sum((needed[:, None, :] & earlier).astype(jnp.int32), axis=2)
    slots = jnp.arange(LANES, dtype=jnp.int32)
    hit = needed[:, None, :] & (rank[:, None, :] == slots[None, :, None])
    wanted = jnp.sum(jnp.where(hit, local[None, None, :], 0), axis=2)

    def exchange(value):
        return lax.all_to_all(value, axes, split_axis=0, concat_axis=0, tiled=True)

    requested = exchange(wanted)
    pool, mh, ml = upward(leaf_density, m2m, box_count // 2)
    chosen = choose(pool, requested, 0, None)
    received = exchange(chosen)

    pair_rank = jnp.sum(jnp.where(named, rank.reshape(-1)[None, :], 0), axis=1)
    mine = owner == device
    source = jnp.where(mine, ids % box_count, owner)
    target = jnp.repeat(jnp.arange(box_count, dtype=jnp.int32), v_source.shape[1])
    codes = v_class.reshape(-1) * 4096 + target * 256 + source
    listing, spans = stage_lists(jnp.where(mine, 0, 1 + pair_rank), codes, 1 + CAP)

    first = (device * (box_count // 8)) % 8
    current = coarse_partial(pool, mh, ml, tie(first.reshape(1).astype(jnp.int32), chosen), rhs)
    group_size = 64 // box_count
    for bit in range(group_size.bit_length() - 1):
        pairs = [(i, i ^ (1 << bit)) for i in range(ndev)]
        current = current + lax.ppermute(current, axes, pairs)
    share = rhs // group_size
    coarse = lax.dynamic_slice_in_dim(current, (device % group_size) * share, share, 1)

    chosen_second = choose(pool, requested, 1, chosen)
    acc = field(pool, None, listing, spans[0], box_count, size, False, chosen_second)
    received_second = exchange(tie(chosen_second, (acc, coarse)))
    acc = field(received, acc, listing, spans[1], box_count, size, False, None)
    out = field(received_second, acc, listing, spans[2], box_count, size, True, None)
    return (coarse, out)


def solution(mesh):
    both = ("row", "col")
    return jax.shard_map(
        body,
        mesh=mesh,
        in_specs=(P(None, both), P(), P(both, None), P(both, None)),
        out_specs=(P(None, both), P(None, both)),
        check_vma=False,
    )
```

```python
import functools
import math

import jax
import jax.numpy as jnp
import numpy as np
from jax import lax
from jax.experimental import pallas as pl
from jax.experimental.pallas import tpu as pltpu
from jax.sharding import PartitionSpec as P

CAP = 2
LANES = 128
KPAD = 384

radius = 0.525
kernel_scale = 1.0 / (4.0 * math.pi)
bf16 = jnp.bfloat16
f32 = jnp.float32


def surface_points(count):
    edge_count = 2
    while edge_count**3 - (edge_count - 2) ** 3 != count:
        edge_count += 1
    coords = np.linspace(-1.0, 1.0, edge_count)
    lattice = np.stack(np.meshgrid(coords, coords, coords, indexing="ij"), -1).reshape(-1, 3)
    border = np.max(np.abs(lattice), axis=1) > 1.0 - 1e-09
    return lattice[border]


def offset_table():
    coords = np.arange(-3, 4)
    lattice = np.stack(np.meshgrid(coords, coords, coords, indexing="ij"), -1).reshape(-1, 3)
    farther = np.max(np.abs(lattice), axis=1) >= 2
    return lattice[farther]


def low_lanes(rows):
    return lax.broadcasted_iota(jnp.int32, (rows, LANES), 1) < LANES // 2


def half_turn(value):
    return pltpu.roll(value, LANES // 2, 1)


def row_tiles(count):
    return [(start, min(16, count - start)) for start in range(0, count, 16)]


def split_store(value, rows, hi_ref, lo_ref, at_row, at_lane, lanes):
    hi = value.astype(bf16)
    lo = (value - hi.astype(f32)).astype(bf16)
    hi_ref[at_row : at_row + rows, at_lane : at_lane + lanes] = hi
    lo_ref[at_row : at_row + rows, at_lane : at_lane + lanes] = lo


def pair_columns(first, second, rows):
    low = low_lanes(rows)
    return (
        jnp.where(low, first, half_turn(second)),
        jnp.where(low, half_turn(first), second),
    )


def three_dots(m_hi, m_lo, x_hi, x_lo):
    out = jnp.dot(m_hi, x_hi, preferred_element_type=f32)
    out = out + jnp.dot(m_lo, x_hi, preferred_element_type=f32)
    return out + jnp.dot(m_hi, x_lo, preferred_element_type=f32)


def upward_kernel(leaf_ref, m_ref, out_ref, mh_ref, ml_ref, xh, xl):
    size = m_ref.shape[1]

    @pl.when(pl.program_id(0) == 0)
    def _():
        mh_ref[...] = jnp.zeros_like(mh_ref)
        ml_ref[...] = jnp.zeros_like(ml_ref)
        xh[...] = jnp.zeros_like(xh)
        xl[...] = jnp.zeros_like(xl)
        for child in range(8):
            for start, rows in row_tiles(size):
                split_store(
                    m_ref[child, start : start + rows, :], rows, mh_ref, ml_ref, start, child * KPAD, size
                )

    for slab in range(out_ref.shape[0]):
        for duo in range(4):
            left = slab * 8 * LANES + duo * LANES
            right = left + 4 * LANES
            for start, rows in row_tiles(size):
                even, odd = pair_columns(
                    leaf_ref[start : start + rows, left : left + LANES],
                    leaf_ref[start : start + rows, right : right + LANES],
                    rows,
                )
                split_store(even, rows, xh, xl, 2 * duo * KPAD + start, slab * LANES, LANES)
                split_store(odd, rows, xh, xl, (2 * duo + 1) * KPAD + start, slab * LANES, LANES)
    out = three_dots(mh_ref[...], ml_ref[...], xh[...], xl[...])
    for slab in range(out_ref.shape[0]):
        out_ref[slab] = out[:, slab * LANES : (slab + 1) * LANES]


def upward(leaf, m2m, slabs):
    size = m2m.shape[1]
    step = 2
    return pl.pallas_call(
        upward_kernel,
        grid=(slabs // step,),
        in_specs=[
            pl.BlockSpec((size, step * 8 * LANES), lambda i: (0, i)),
            pl.BlockSpec(m2m.shape, lambda i: (0, 0, 0)),
        ],
        out_specs=[
            pl.BlockSpec((step, size, LANES), lambda i: (i, 0, 0)),
            pl.BlockSpec((size, 8 * KPAD), lambda i: (0, 0)),
            pl.BlockSpec((size, 8 * KPAD), lambda i: (0, 0)),
        ],
        out_shape=[
            jax.ShapeDtypeStruct((slabs, size, LANES), f32),
            jax.ShapeDtypeStruct((size, 8 * KPAD), bf16),
            jax.ShapeDtypeStruct((size, 8 * KPAD), bf16),
        ],
        scratch_shapes=[
            pltpu.VMEM((8 * KPAD, step * LANES), bf16),
            pltpu.VMEM((8 * KPAD, step * LANES), bf16),
        ],
        cost_estimate=pl.CostEstimate(
            flops=2 * 8 * size * size * slabs * LANES * 3,
            bytes_accessed=4 * (leaf.size + m2m.size),
            transcendentals=0,
        ),
        name="upward",
    )(leaf, m2m)


def coarse_kernel(first_ref, pool_ref, mh_ref, ml_ref, out_ref, xh, xl, yh, yl):
    size = out_ref.shape[0]
    for ref in (xh, xl, yh, yl):
        ref[...] = jnp.zeros_like(ref)
    for duo in range(4):
        for start, rows in row_tiles(size):
            even, odd = pair_columns(
                pool_ref[duo, start : start + rows, :], pool_ref[4 + duo, start : start + rows, :], rows
            )
            split_store(even, rows, xh, xl, 2 * duo * KPAD + start, 0, LANES)
            split_store(odd, rows, xh, xl, (2 * duo + 1) * KPAD + start, 0, LANES)
    upper = three_dots(mh_ref[...], ml_ref[...], xh[...], xl[...])
    for start, rows in row_tiles(size):
        part = upper[start : start + rows]
        low = low_lanes(rows)
        split_store(jnp.where(low, part, 0.0), rows, yh, yl, start, 0, LANES)
        split_store(jnp.where(low, half_turn(part), 0.0), rows, yh, yl, KPAD + start, 0, LANES)
    at = pl.multiple_of(first_ref[0] * KPAD, LANES)
    out = three_dots(
        mh_ref[:, pl.ds(at, 2 * KPAD)], ml_ref[:, pl.ds(at, 2 * KPAD)], yh[...], yl[...]
    )
    out_ref[...] = out[:, : out_ref.shape[1]]


def coarse_partial(pool, mh, ml, first, rhs):
    slabs, size, _ = pool.shape
    vmem = pl.BlockSpec(memory_space=pltpu.VMEM)
    return pl.pallas_call(
        coarse_kernel,
        in_specs=[pl.BlockSpec(memory_space=pltpu.SMEM), vmem, vmem, vmem],
        out_specs=vmem,
        out_shape=jax.ShapeDtypeStruct((size, rhs), f32),
        scratch_shapes=[
            pltpu.VMEM((8 * KPAD, LANES), bf16),
            pltpu.VMEM((8 * KPAD, LANES), bf16),
            pltpu.VMEM((2 * KPAD, LANES), bf16),
            pltpu.VMEM((2 * KPAD, LANES), bf16),
        ],
        cost_estimate=pl.CostEstimate(
            flops=2 * 8 * size * size * 2 * LANES * 3,
            bytes_accessed=4 * pool.size + 4 * mh.size,
            transcendentals=0,
        ),
        name="coarse",
    )(first, pool, mh, ml)


def fold_rows(size):
    first = size // 2 // 16 * 16
    return first, size - first


def choose_kernel(count, slot, wanted_ref, pool_ref, out_ref, ready, sems):
    size = pool_ref.shape[1]
    upper, lower = fold_rows(size)

    def send(dest):
        return pltpu.make_async_copy(ready.at[dest], out_ref.at[dest], sems.at[dest])

    @pl.loop(0, count, unroll=4)
    def _(dest):
        box = wanted_ref[dest, slot]
        slab = lax.shift_right_logical(box, 1)
        odd = (box & 1) == 1
        for start, rows in row_tiles(lower):
            under = pool_ref[slab, upper + start : upper + start + rows, :]
            have = min(rows, upper - start)
            if have <= 0:
                over = jnp.zeros_like(under)
            else:
                over = pool_ref[slab, start : start + have, :]
                if have < rows:
                    over = jnp.concatenate([over, jnp.zeros((rows - have, LANES), f32)], axis=0)
            turned = half_turn(jnp.where(odd, over, under))
            low = low_lanes(rows)
            ready[dest, start : start + rows, :] = jnp.where(
                odd, jnp.where(low, turned, under), jnp.where(low, over, turned)
            )
        send(dest).start()

    for dest in range(count):
        send(dest).wait()


def choose(pool, wanted, slot, after):
    dests = wanted.shape[0]
    size = pool.shape[1]
    shape = (dests, fold_rows(size)[1], LANES)
    return pl.pallas_call(
        functools.partial(choose_kernel, dests, slot),
        in_specs=[pl.BlockSpec(memory_space=pltpu.SMEM), pl.BlockSpec(memory_space=pltpu.VMEM)],
        out_specs=pl.BlockSpec(memory_space=pl.ANY),
        out_shape=jax.ShapeDtypeStruct(shape, f32),
        scratch_shapes=[pltpu.VMEM(shape, f32), pltpu.SemaphoreType.DMA((dests,))],
        cost_estimate=pl.CostEstimate(
            flops=0, bytes_accessed=4 * (pool.size + math.prod(shape)), transcendentals=0
        ),
        name="choose",
    )(tie(wanted, after), pool)


def tie(value, after):
    return value if after is None else lax.optimization_barrier((value, after))[0]


MAIN = 256
TAIL = 64


def field_kernel(
    first, last, boxes, size, tbl_ref, list_ref, span_ref, there_ref, col_ref, row_ref, pool_hbm, *rest
):
    rest = list(rest)
    acc_hbm = None if first else rest.pop(0)
    out_ref, acc, pool_ref, sp, dist, arrived, carried, *done = rest
    slabs, held, _ = pool_ref.shape
    upper, lower = fold_rows(size)
    folded = held != size
    rows_pad = dist.shape[0]

    def fetch(slab):
        return pltpu.make_async_copy(pool_hbm.at[slab], pool_ref.at[slab], arrived.at[slab])

    for slab in range(slabs):
        pl.when(there_ref[slab] > 0)(fetch(slab).start)
    if first:
        acc[...] = jnp.zeros_like(acc)
    else:
        acc_copy = pltpu.make_async_copy(acc_hbm, acc, carried)
        acc_copy.start()

    for start, rows in row_tiles(rows_pad):
        for lane in range(0, KPAD, LANES):
            total = jnp.zeros((rows, LANES), f32)
            for comp in range(3):
                delta = (
                    col_ref[comp, start : start + rows, :] - row_ref[comp : comp + 1, lane : lane + LANES]
                )
                total = total + delta * delta
            dist[start : start + rows, lane : lane + LANES] = total

    def prepare(slab):
        fetch(slab).wait()

        def keep(source, at, value):
            lesser = value - value.astype(bf16).astype(f32)
            sp[source, at : at + value.shape[0], :] = jnp.where(
                low_lanes(value.shape[0]), value, lesser
            ).astype(bf16)

        def empty(source, at):
            rows = MAIN + TAIL - at
            sp[source, at : at + rows, :] = jnp.zeros((rows, LANES), bf16)

        for start, rows in row_tiles(held):
            value = pool_ref[slab, start : start + rows, :]
            if rows < 16:
                value = jnp.concatenate([value, jnp.zeros((16 - rows, LANES), f32)], axis=0)
            low = low_lanes(16)
            turned = half_turn(value)
            left, right = jnp.where(low, value, turned), jnp.where(low, turned, value)
            if folded:
                if start < upper:
                    keep(slab, start, left)
                keep(slab, upper + start, right)
            else:
                keep(2 * slab, start, left)
                keep(2 * slab + 1, start, right)
        ending = -(-size // 16) * 16
        for source in (slab,) if folded else (2 * slab, 2 * slab + 1):
            empty(source, ending)

    @pl.loop(0, slabs)
    def _(slab):
        pl.when(there_ref[slab] > 0)(functools.partial(prepare, slab))

    if not first:
        acc_copy.wait()
    begin = span_ref[0]
    count = span_ref[1]

    def read(index):
        code = list_ref[begin + jnp.minimum(index, count - 1)]
        cls = lax.shift_right_logical(code, 12)
        source = code & 255
        target = jnp.where(index < count, lax.shift_right_logical(code, 8) & 15, boxes)
        return [tbl_ref[cls * 3 + comp] for comp in range(3)], source, target

    def duo(index, sums):
        members = [read(index), read(index + 1)]
        shifts, twice = [], []
        for offset, _, _ in members:
            base = offset[0] * offset[0] + offset[1] * offset[1] + offset[2] * offset[2]
            double = [2.0 * comp for comp in offset]
            twice.append(double)
            shifts.append(
                double[0] * row_ref[0:1, :] + double[1] * row_ref[1:2, :] + double[2] * row_ref[2:3, :] + base
            )
        low = low_lanes(16)
        shift_tail = jnp.where(low[:1], shifts[0][:, MAIN:], shifts[1][:, MAIN:])
        tiles = []
        for start, rows in row_tiles(rows_pad):
            point = [col_ref[comp, start : start + rows, :] for comp in range(3)]
            owns = [d[0] * point[0] + d[1] * point[1] + d[2] * point[2] for d in twice]
            parts = []
            for own, shift in zip(owns, shifts):
                own = jnp.concatenate([own, own], axis=1)
                value = lax.rsqrt(dist[start : start + rows, :MAIN] + (shift[:, :MAIN] - own))
                hi = value.astype(bf16)
                parts += [hi, (value - hi.astype(f32)).astype(bf16)]
            own = jnp.where(low, owns[0], owns[1])
            value = lax.rsqrt(dist[start : start + rows, MAIN:] + (shift_tail - own))
            hi = value.astype(bf16)
            parts.append(jnp.concatenate([hi, (value - hi.astype(f32)).astype(bf16)], axis=1))
            tiles.append(parts)

        mains, tails = [], []
        for at, (_, source, _) in enumerate(members):
            for begin_row, rows, kept in ((0, MAIN, mains), (MAIN, TAIL, tails)):
                part = sp[source, begin_row : begin_row + rows, :]
                empty = jnp.zeros_like(part)
                kept.append(jnp.concatenate([part, empty] if at == 0 else [empty, part], axis=1))
        stationary = [mains[0], mains[0], mains[1], mains[1], jnp.concatenate(tails * 2, axis=0)]
        for chunk, rhs in enumerate(stationary):
            fresh = chunk not in (1, 3)
            for unit in range(2):
                if fresh:
                    pltpu.matmul_push_rhs(rhs, 0, unit)
                for at in range(unit, len(tiles), 2):
                    pltpu.matmul_acc_lhs(sums[at], tiles[at][chunk], 0 if at == unit and fresh else None)
        for at, (start, rows) in enumerate(row_tiles(rows_pad)):
            have = min(rows, size - start)
            product = pltpu.matmul_pop(sums[at])
            for number, (_, _, target) in enumerate(members):
                mine = product[:have, number * LANES : (number + 1) * LANES]
                acc[target, start : start + have, :] = acc[target, start : start + have, :] + mine

    def duos(*flat):
        sums = flat[: len(flat) // 2], flat[len(flat) // 2 :]

        whole = lax.shift_right_logical(count, 3)

        @pl.loop(0, whole)
        def _(step):
            for half in range(4):
                duo(8 * step + 2 * half, sums[half % 2])

        @pl.loop(4 * whole, lax.shift_right_logical(count + 1, 1))
        def _(step):
            duo(2 * step, sums[0])

    tiles_of = enumerate(row_tiles(rows_pad))
    kinds = [pltpu.ACC(at % 2)((rows, 256), f32) for at, (_, rows) in tiles_of]
    pl.run_scoped(duos, *kinds, *kinds)

    if not last:
        result = pltpu.make_async_copy(acc, out_ref, carried)
        result.start()
        result.wait()
    else:
        ready, sems = done

        def send(slab):
            lanes = pl.ds(slab * LANES, LANES)
            return pltpu.make_async_copy(ready.at[:, lanes], out_ref.at[:, lanes], sems.at[slab])

        for slab in range(boxes // 2):
            for start, rows in row_tiles(size):
                left = acc[2 * slab, start : start + rows, :]
                right = acc[2 * slab + 1, start : start + rows, :]
                ready[start : start + rows, slab * LANES : (slab + 1) * LANES] = kernel_scale * jnp.where(
                    low_lanes(rows), left + half_turn(left), right + half_turn(right)
                )
            send(slab).start()
        for slab in range(boxes // 2):
            send(slab).wait()


def field(pool, acc, listing, span, there, boxes, size, last, after):
    slabs, held, _ = pool.shape
    sources = slabs if held != size else 2 * slabs
    points = surface_points(size) * radius
    rows_pad = -(-size // 16) * 16
    col = np.zeros((3, rows_pad, LANES), np.float32)
    col[:, :size] = points.T[:, :, None]
    row = np.zeros((8, KPAD), np.float32)
    row[:3, :size] = points.T
    row[:, MAIN + TAIL :] = row[:, MAIN : MAIN + TAIL]
    vmem = pl.BlockSpec(memory_space=pltpu.VMEM)
    smem = pl.BlockSpec(memory_space=pltpu.SMEM)
    first = acc is None
    args = [jnp.asarray(offset_table().reshape(-1), f32), listing, tie(span, after), there, jnp.asarray(col), jnp.asarray(row), pool]
    hbm = pl.BlockSpec(memory_space=pltpu.HBM)
    specs = [smem, smem, smem, smem, vmem, vmem, hbm]
    sums = (boxes + 1, size, LANES)
    scratch = [
        pltpu.VMEM(sums, f32),
        pltpu.VMEM(pool.shape, f32),
        pltpu.VMEM((sources, MAIN + TAIL, LANES), bf16),
        pltpu.VMEM((rows_pad, KPAD), f32),
        pltpu.SemaphoreType.DMA((slabs,)),
        pltpu.SemaphoreType.DMA,
    ]
    if last:
        scratch += [
            pltpu.VMEM((size, boxes * LANES // 2), f32),
            pltpu.SemaphoreType.DMA((boxes // 2,)),
        ]
    if not first:
        args.append(acc)
        specs.append(hbm)
    pairs = listing.shape[0] // 3
    return pl.pallas_call(
        functools.partial(field_kernel, first, last, boxes, size),
        in_specs=specs,
        out_specs=pl.BlockSpec(memory_space=pl.ANY) if last else hbm,
        out_shape=jax.ShapeDtypeStruct((size, boxes * LANES // 2) if last else sums, f32),
        scratch_shapes=scratch,
        compiler_params=pltpu.CompilerParams(vmem_limit_bytes=67043328),
        cost_estimate=pl.CostEstimate(
            flops=2 * rows_pad * 2 * KPAD * LANES * pairs,
            bytes_accessed=4 * pool.size,
            transcendentals=rows_pad * KPAD * pairs,
        ),
        name="field",
    )(*args)


def stage_lists(stage, codes, stages):
    slots = codes.shape[0]
    order = jnp.arange(slots, dtype=jnp.int32)
    ahead = (stage[None, :] < stage[:, None]) | (
        (stage[None, :] == stage[:, None]) & (order[None, :] < order[:, None])
    )
    place = jnp.sum(ahead.astype(jnp.int32), axis=1)
    listing = jnp.sum(jnp.where(place[None, :] == order[:, None], codes[None, :], 0), axis=1)
    numbers = jnp.arange(stages, dtype=jnp.int32)
    counts = jnp.sum((stage[None, :] == numbers[:, None]).astype(jnp.int32), axis=1)
    begins = jnp.sum((stage[None, :] < numbers[:, None]).astype(jnp.int32), axis=1)
    return listing, jnp.stack([begins, counts], axis=1)


def body(leaf_density, m2m, v_source, v_class):
    axes = ("row", "col")
    size = m2m.shape[1]
    box_count = v_source.shape[0]
    rhs = leaf_density.shape[1] // (8 * box_count)
    device, ndev = lax.axis_index(axes), lax.axis_size(axes)

    ids = v_source.reshape(-1)
    owner = ids // box_count
    named = ids[:, None] == jnp.arange(ndev * box_count, dtype=jnp.int32)[None, :]
    needed = jnp.any(named, axis=0).reshape(ndev, box_count)
    local = jnp.arange(box_count, dtype=jnp.int32)
    earlier = (local[None, :] < local[:, None])[None]
    rank = jnp.sum((needed[:, None, :] & earlier).astype(jnp.int32), axis=2)
    slots = jnp.arange(LANES, dtype=jnp.int32)
    hit = needed[:, None, :] & (rank[:, None, :] == slots[None, :, None])
    wanted = jnp.sum(jnp.where(hit, local[None, None, :], 0), axis=2)

    def exchange(value):
        return lax.all_to_all(value, axes, split_axis=0, concat_axis=0, tiled=True)

    requested = exchange(wanted)
    pool, mh, ml = upward(leaf_density, m2m, box_count // 2)
    chosen = choose(pool, requested, 0, None)
    received = exchange(chosen)

    pair_rank = jnp.sum(jnp.where(named, rank.reshape(-1)[None, :], 0), axis=1)
    mine = owner == device
    source = jnp.where(mine, ids % box_count, owner)
    target = jnp.repeat(jnp.arange(box_count, dtype=jnp.int32), v_source.shape[1])
    codes = v_class.reshape(-1) * 4096 + target * 256 + source
    listing, spans = stage_lists(jnp.where(mine, 0, 1 + pair_rank), codes, 1 + CAP)

    first = (device * (box_count // 8)) % 8
    current = coarse_partial(pool, mh, ml, tie(first.reshape(1).astype(jnp.int32), chosen), rhs)
    group_size = 64 // box_count
    for bit in range(group_size.bit_length() - 1):
        pairs = [(i, i ^ (1 << bit)) for i in range(ndev)]
        current = current + lax.ppermute(current, axes, pairs)
    share = rhs // group_size
    coarse = lax.dynamic_slice_in_dim(current, (device % group_size) * share, share, 1)

    chosen_second = choose(pool, requested, 1, chosen)
    there = jnp.sum(needed.astype(jnp.int32), axis=1)
    every = jnp.ones((box_count // 2,), jnp.int32)
    acc = field(pool, None, listing, spans[0], every, box_count, size, False, chosen_second)
    received_second = exchange(tie(chosen_second, (acc, coarse)))
    acc = field(received, acc, listing, spans[1], there, box_count, size, False, None)
    out = field(received_second, acc, listing, spans[2], there - 1, box_count, size, True, None)
    return (coarse, out)


def solution(mesh):
    both = ("row", "col")
    return jax.shard_map(
        body,
        mesh=mesh,
        in_specs=(P(None, both), P(), P(both, None), P(both, None)),
        out_specs=(P(None, both), P(None, both)),
        check_vma=False,
    )
```

```python
import functools
import math

import jax
import jax.numpy as jnp
import numpy as np
from jax import lax
from jax.experimental import pallas as pl
from jax.experimental.pallas import tpu as pltpu
from jax.sharding import PartitionSpec as P

CAP = 2
LANES = 128
KPAD = 384

radius = 0.525
kernel_scale = 1.0 / (4.0 * math.pi)
bf16 = jnp.bfloat16
f32 = jnp.float32


def surface_points(count):
    edge_count = 2
    while edge_count**3 - (edge_count - 2) ** 3 != count:
        edge_count += 1
    coords = np.linspace(-1.0, 1.0, edge_count)
    lattice = np.stack(np.meshgrid(coords, coords, coords, indexing="ij"), -1).reshape(-1, 3)
    border = np.max(np.abs(lattice), axis=1) > 1.0 - 1e-09
    return lattice[border]


def offset_table():
    coords = np.arange(-3, 4)
    lattice = np.stack(np.meshgrid(coords, coords, coords, indexing="ij"), -1).reshape(-1, 3)
    farther = np.max(np.abs(lattice), axis=1) >= 2
    return lattice[farther]


def low_lanes(rows):
    return lax.broadcasted_iota(jnp.int32, (rows, LANES), 1) < LANES // 2


def half_turn(value):
    return pltpu.roll(value, LANES // 2, 1)


def row_tiles(count):
    return [(start, min(16, count - start)) for start in range(0, count, 16)]


def split_store(value, rows, hi_ref, lo_ref, at_row, at_lane, lanes):
    hi = value.astype(bf16)
    lo = (value - hi.astype(f32)).astype(bf16)
    hi_ref[at_row : at_row + rows, at_lane : at_lane + lanes] = hi
    lo_ref[at_row : at_row + rows, at_lane : at_lane + lanes] = lo


def pair_columns(first, second, rows):
    low = low_lanes(rows)
    return (
        jnp.where(low, first, half_turn(second)),
        jnp.where(low, half_turn(first), second),
    )


def three_dots(m_hi, m_lo, x_hi, x_lo):
    out = jnp.dot(m_hi, x_hi, preferred_element_type=f32)
    out = out + jnp.dot(m_lo, x_hi, preferred_element_type=f32)
    return out + jnp.dot(m_hi, x_lo, preferred_element_type=f32)


def upward_kernel(leaf_ref, m_ref, out_ref, mh_ref, ml_ref, xh, xl):
    size = m_ref.shape[1]

    @pl.when(pl.program_id(0) == 0)
    def _():
        lane, line = size // LANES * LANES, size // 16 * 16
        for child in range(8):
            for ref in (mh_ref, ml_ref):
                ref[:, child * KPAD + lane : (child + 1) * KPAD] = jnp.zeros((size, KPAD - lane), bf16)
            for ref in (xh, xl):
                ref[child * KPAD + line : (child + 1) * KPAD, :] = jnp.zeros(
                    (KPAD - line, ref.shape[1]), bf16
                )
            for start, rows in row_tiles(size):
                split_store(
                    m_ref[child, start : start + rows, :], rows, mh_ref, ml_ref, start, child * KPAD, size
                )

    for slab in range(out_ref.shape[0]):
        for duo in range(4):
            left = slab * 8 * LANES + duo * LANES
            right = left + 4 * LANES
            for start, rows in row_tiles(size):
                even, odd = pair_columns(
                    leaf_ref[start : start + rows, left : left + LANES],
                    leaf_ref[start : start + rows, right : right + LANES],
                    rows,
                )
                split_store(even, rows, xh, xl, 2 * duo * KPAD + start, slab * LANES, LANES)
                split_store(odd, rows, xh, xl, (2 * duo + 1) * KPAD + start, slab * LANES, LANES)
    out = three_dots(mh_ref[...], ml_ref[...], xh[...], xl[...])
    for slab in range(out_ref.shape[0]):
        out_ref[slab] = out[:, slab * LANES : (slab + 1) * LANES]


def upward(leaf, m2m, slabs):
    size = m2m.shape[1]
    step = 2
    return pl.pallas_call(
        upward_kernel,
        grid=(slabs // step,),
        in_specs=[
            pl.BlockSpec((size, step * 8 * LANES), lambda i: (0, i)),
            pl.BlockSpec(m2m.shape, lambda i: (0, 0, 0)),
        ],
        out_specs=[
            pl.BlockSpec((step, size, LANES), lambda i: (i, 0, 0)),
            pl.BlockSpec((size, 8 * KPAD), lambda i: (0, 0)),
            pl.BlockSpec((size, 8 * KPAD), lambda i: (0, 0)),
        ],
        out_shape=[
            jax.ShapeDtypeStruct((slabs, size, LANES), f32),
            jax.ShapeDtypeStruct((size, 8 * KPAD), bf16),
            jax.ShapeDtypeStruct((size, 8 * KPAD), bf16),
        ],
        scratch_shapes=[
            pltpu.VMEM((8 * KPAD, step * LANES), bf16),
            pltpu.VMEM((8 * KPAD, step * LANES), bf16),
        ],
        cost_estimate=pl.CostEstimate(
            flops=2 * 8 * size * size * slabs * LANES * 3,
            bytes_accessed=4 * (leaf.size + m2m.size),
            transcendentals=0,
        ),
        name="upward",
    )(leaf, m2m)


def coarse_kernel(first_ref, pool_ref, mh_ref, ml_ref, out_ref, xh, xl, yh, yl):
    size = out_ref.shape[0]
    for ref in (xh, xl, yh, yl):
        ref[...] = jnp.zeros_like(ref)
    for duo in range(4):
        for start, rows in row_tiles(size):
            even, odd = pair_columns(
                pool_ref[duo, start : start + rows, :], pool_ref[4 + duo, start : start + rows, :], rows
            )
            split_store(even, rows, xh, xl, 2 * duo * KPAD + start, 0, LANES)
            split_store(odd, rows, xh, xl, (2 * duo + 1) * KPAD + start, 0, LANES)
    upper = three_dots(mh_ref[...], ml_ref[...], xh[...], xl[...])
    for start, rows in row_tiles(size):
        part = upper[start : start + rows]
        low = low_lanes(rows)
        split_store(jnp.where(low, part, 0.0), rows, yh, yl, start, 0, LANES)
        split_store(jnp.where(low, half_turn(part), 0.0), rows, yh, yl, KPAD + start, 0, LANES)
    at = pl.multiple_of(first_ref[0] * KPAD, LANES)
    out = three_dots(
        mh_ref[:, pl.ds(at, 2 * KPAD)], ml_ref[:, pl.ds(at, 2 * KPAD)], yh[...], yl[...]
    )
    out_ref[...] = out[:, : out_ref.shape[1]]


def coarse_partial(pool, mh, ml, first, rhs):
    slabs, size, _ = pool.shape
    vmem = pl.BlockSpec(memory_space=pltpu.VMEM)
    return pl.pallas_call(
        coarse_kernel,
        in_specs=[pl.BlockSpec(memory_space=pltpu.SMEM), vmem, vmem, vmem],
        out_specs=vmem,
        out_shape=jax.ShapeDtypeStruct((size, rhs), f32),
        scratch_shapes=[
            pltpu.VMEM((8 * KPAD, LANES), bf16),
            pltpu.VMEM((8 * KPAD, LANES), bf16),
            pltpu.VMEM((2 * KPAD, LANES), bf16),
            pltpu.VMEM((2 * KPAD, LANES), bf16),
        ],
        cost_estimate=pl.CostEstimate(
            flops=2 * 8 * size * size * 2 * LANES * 3,
            bytes_accessed=4 * pool.size + 4 * mh.size,
            transcendentals=0,
        ),
        name="coarse",
    )(first, pool, mh, ml)


def fold_rows(size):
    first = size // 2 // 16 * 16
    return first, size - first


def choose_kernel(count, slot, wanted_ref, pool_ref, out_ref, ready, sems):
    size = pool_ref.shape[1]
    upper, lower = fold_rows(size)

    def send(dest):
        return pltpu.make_async_copy(ready.at[dest], out_ref.at[dest], sems.at[dest])

    @pl.loop(0, count, unroll=8)
    def _(dest):
        box = wanted_ref[dest, slot]
        slab = lax.shift_right_logical(box, 1)
        odd = (box & 1) == 1
        for start, rows in row_tiles(lower):
            under = pool_ref[slab, upper + start : upper + start + rows, :]
            have = min(rows, upper - start)
            if have <= 0:
                over = jnp.zeros_like(under)
            else:
                over = pool_ref[slab, start : start + have, :]
                if have < rows:
                    over = jnp.concatenate([over, jnp.zeros((rows - have, LANES), f32)], axis=0)
            turned = half_turn(jnp.where(odd, over, under))
            low = low_lanes(rows)
            ready[dest, start : start + rows, :] = jnp.where(
                odd, jnp.where(low, turned, under), jnp.where(low, over, turned)
            )
        send(dest).start()

    for dest in range(count):
        send(dest).wait()


def choose(pool, wanted, slot, after):
    dests = wanted.shape[0]
    size = pool.shape[1]
    shape = (dests, fold_rows(size)[1], LANES)
    return pl.pallas_call(
        functools.partial(choose_kernel, dests, slot),
        in_specs=[pl.BlockSpec(memory_space=pltpu.SMEM), pl.BlockSpec(memory_space=pltpu.VMEM)],
        out_specs=pl.BlockSpec(memory_space=pl.ANY),
        out_shape=jax.ShapeDtypeStruct(shape, f32),
        scratch_shapes=[pltpu.VMEM(shape, f32), pltpu.SemaphoreType.DMA((dests,))],
        cost_estimate=pl.CostEstimate(
            flops=0, bytes_accessed=4 * (pool.size + math.prod(shape)), transcendentals=0
        ),
        name="choose",
    )(tie(wanted, after), pool)


def tie(value, after):
    return value if after is None else lax.optimization_barrier((value, after))[0]


MAIN = 256
TAIL = 64


def field_kernel(
    first, last, boxes, size, tbl_ref, list_ref, span_ref, there_ref, col_ref, row_ref, pool_hbm, *rest
):
    rest = list(rest)
    acc_hbm = None if first else rest.pop(0)
    out_ref, acc, pool_ref, sp, dist, arrived, carried, *done = rest
    slabs, held, _ = pool_ref.shape
    upper, lower = fold_rows(size)
    folded = held != size
    rows_pad = dist.shape[0]

    def fetch(slab):
        return pltpu.make_async_copy(pool_hbm.at[slab], pool_ref.at[slab], arrived.at[slab])

    for slab in range(slabs):
        pl.when(there_ref[slab] > 0)(fetch(slab).start)
    if first:
        acc[...] = jnp.zeros_like(acc)
    else:
        acc_copy = pltpu.make_async_copy(acc_hbm, acc, carried)
        acc_copy.start()

    for start, rows in row_tiles(rows_pad):
        for lane in range(0, KPAD, LANES):
            total = jnp.zeros((rows, LANES), f32)
            for comp in range(3):
                delta = (
                    col_ref[comp, start : start + rows, :] - row_ref[comp : comp + 1, lane : lane + LANES]
                )
                total = total + delta * delta
            dist[start : start + rows, lane : lane + LANES] = total

    def prepare(slab):
        fetch(slab).wait()

        def keep(source, at, value):
            lesser = value - value.astype(bf16).astype(f32)
            sp[source, at : at + value.shape[0], :] = jnp.where(
                low_lanes(value.shape[0]), value, lesser
            ).astype(bf16)

        def empty(source, at):
            rows = MAIN + TAIL - at
            sp[source, at : at + rows, :] = jnp.zeros((rows, LANES), bf16)

        for start, rows in row_tiles(held):
            value = pool_ref[slab, start : start + rows, :]
            if rows < 16:
                value = jnp.concatenate([value, jnp.zeros((16 - rows, LANES), f32)], axis=0)
            low = low_lanes(16)
            turned = half_turn(value)
            left, right = jnp.where(low, value, turned), jnp.where(low, turned, value)
            if folded:
                if start < upper:
                    keep(slab, start, left)
                keep(slab, upper + start, right)
            else:
                keep(2 * slab, start, left)
                keep(2 * slab + 1, start, right)
        ending = -(-size // 16) * 16
        for source in (slab,) if folded else (2 * slab, 2 * slab + 1):
            empty(source, ending)

    @pl.loop(0, slabs)
    def _(slab):
        pl.when(there_ref[slab] > 0)(functools.partial(prepare, slab))

    if not first:
        acc_copy.wait()
    begin = span_ref[0]
    count = span_ref[1]

    def read(index):
        code = list_ref[begin + jnp.minimum(index, count - 1)]
        cls = lax.shift_right_logical(code, 12)
        source = code & 255
        target = jnp.where(index < count, lax.shift_right_logical(code, 8) & 15, boxes)
        return [tbl_ref[cls * 3 + comp] for comp in range(3)], source, target

    def duo(index, sums):
        members = [read(index), read(index + 1)]
        shifts, twice = [], []
        for offset, _, _ in members:
            base = offset[0] * offset[0] + offset[1] * offset[1] + offset[2] * offset[2]
            double = [2.0 * comp for comp in offset]
            twice.append(double)
            shifts.append(
                double[0] * row_ref[0:1, :] + double[1] * row_ref[1:2, :] + double[2] * row_ref[2:3, :] + base
            )
        low = low_lanes(16)
        shift_tail = jnp.where(low[:1], shifts[0][:, MAIN:], shifts[1][:, MAIN:])
        tiles = []
        for start, rows in row_tiles(rows_pad):
            point = [col_ref[comp, start : start + rows, :] for comp in range(3)]
            owns = [d[0] * point[0] + d[1] * point[1] + d[2] * point[2] for d in twice]
            parts = []
            for own, shift in zip(owns, shifts):
                own = jnp.concatenate([own, own], axis=1)
                value = lax.rsqrt(dist[start : start + rows, :MAIN] + (shift[:, :MAIN] - own))
                hi = value.astype(bf16)
                parts += [hi, (value - hi.astype(f32)).astype(bf16)]
            own = jnp.where(low, owns[0], owns[1])
            value = lax.rsqrt(dist[start : start + rows, MAIN:] + (shift_tail - own))
            hi = value.astype(bf16)
            parts.append(jnp.concatenate([hi, (value - hi.astype(f32)).astype(bf16)], axis=1))
            tiles.append(parts)

        mains, tails = [], []
        for at, (_, source, _) in enumerate(members):
            for begin_row, rows, kept in ((0, MAIN, mains), (MAIN, TAIL, tails)):
                part = sp[source, begin_row : begin_row + rows, :]
                empty = jnp.zeros_like(part)
                kept.append(jnp.concatenate([part, empty] if at == 0 else [empty, part], axis=1))
        stationary = [mains[0], mains[0], mains[1], mains[1], jnp.concatenate(tails * 2, axis=0)]
        for chunk, rhs in enumerate(stationary):
            fresh = chunk not in (1, 3)
            for unit in range(2):
                if fresh:
                    pltpu.matmul_push_rhs(rhs, 0, unit)
                for at in range(unit, len(tiles), 2):
                    pltpu.matmul_acc_lhs(sums[at], tiles[at][chunk], 0 if at == unit and fresh else None)
        for at, (start, rows) in enumerate(row_tiles(rows_pad)):
            have = min(rows, size - start)
            product = pltpu.matmul_pop(sums[at])
            for number, (_, _, target) in enumerate(members):
                mine = product[:have, number * LANES : (number + 1) * LANES]
                acc[target, start : start + have, :] = acc[target, start : start + have, :] + mine

    def duos(*flat):
        sums = flat[: len(flat) // 2], flat[len(flat) // 2 :]

        whole = lax.shift_right_logical(count, 3)

        @pl.loop(0, whole)
        def _(step):
            for half in range(4):
                duo(8 * step + 2 * half, sums[half % 2])

        @pl.loop(4 * whole, lax.shift_right_logical(count + 1, 1))
        def _(step):
            duo(2 * step, sums[0])

    tiles_of = enumerate(row_tiles(rows_pad))
    kinds = [pltpu.ACC(at % 2)((rows, 256), f32) for at, (_, rows) in tiles_of]
    pl.run_scoped(duos, *kinds, *kinds)

    if not last:
        result = pltpu.make_async_copy(acc, out_ref, carried)
        result.start()
        result.wait()
    else:
        ready, sems = done

        def send(slab):
            lanes = pl.ds(slab * LANES, LANES)
            return pltpu.make_async_copy(ready.at[:, lanes], out_ref.at[:, lanes], sems.at[slab])

        for slab in range(boxes // 2):
            for start, rows in row_tiles(size):
                left = acc[2 * slab, start : start + rows, :]
                right = acc[2 * slab + 1, start : start + rows, :]
                ready[start : start + rows, slab * LANES : (slab + 1) * LANES] = kernel_scale * jnp.where(
                    low_lanes(rows), left + half_turn(left), right + half_turn(right)
                )
            send(slab).start()
        for slab in range(boxes // 2):
            send(slab).wait()


def field(pool, acc, listing, span, there, boxes, size, last, after):
    slabs, held, _ = pool.shape
    sources = slabs if held != size else 2 * slabs
    points = surface_points(size) * radius
    rows_pad = -(-size // 16) * 16
    col = np.zeros((3, rows_pad, LANES), np.float32)
    col[:, :size] = points.T[:, :, None]
    row = np.zeros((8, KPAD), np.float32)
    row[:3, :size] = points.T
    row[:, MAIN + TAIL :] = row[:, MAIN : MAIN + TAIL]
    vmem = pl.BlockSpec(memory_space=pltpu.VMEM)
    smem = pl.BlockSpec(memory_space=pltpu.SMEM)
    first = acc is None
    args = [jnp.asarray(offset_table().reshape(-1), f32), listing, tie(span, after), there, jnp.asarray(col), jnp.asarray(row), pool]
    hbm = pl.BlockSpec(memory_space=pltpu.HBM)
    specs = [smem, smem, smem, smem, vmem, vmem, hbm]
    sums = (boxes + 1, size, LANES)
    scratch = [
        pltpu.VMEM(sums, f32),
        pltpu.VMEM(pool.shape, f32),
        pltpu.VMEM((sources, MAIN + TAIL, LANES), bf16),
        pltpu.VMEM((rows_pad, KPAD), f32),
        pltpu.SemaphoreType.DMA((slabs,)),
        pltpu.SemaphoreType.DMA,
    ]
    if last:
        scratch += [
            pltpu.VMEM((size, boxes * LANES // 2), f32),
            pltpu.SemaphoreType.DMA((boxes // 2,)),
        ]
    if not first:
        args.append(acc)
        specs.append(hbm)
    pairs = listing.shape[0] // 3
    return pl.pallas_call(
        functools.partial(field_kernel, first, last, boxes, size),
        in_specs=specs,
        out_specs=pl.BlockSpec(memory_space=pl.ANY) if last else hbm,
        out_shape=jax.ShapeDtypeStruct((size, boxes * LANES // 2) if last else sums, f32),
        scratch_shapes=scratch,
        compiler_params=pltpu.CompilerParams(vmem_limit_bytes=67043328),
        cost_estimate=pl.CostEstimate(
            flops=2 * rows_pad * 2 * KPAD * LANES * pairs,
            bytes_accessed=4 * pool.size,
            transcendentals=rows_pad * KPAD * pairs,
        ),
        name="field",
    )(*args)


def stage_lists(stage, codes, stages):
    slots = codes.shape[0]
    order = jnp.arange(slots, dtype=jnp.int32)
    ahead = (stage[None, :] < stage[:, None]) | (
        (stage[None, :] == stage[:, None]) & (order[None, :] < order[:, None])
    )
    place = jnp.sum(ahead.astype(jnp.int32), axis=1)
    listing = jnp.sum(jnp.where(place[None, :] == order[:, None], codes[None, :], 0), axis=1)
    numbers = jnp.arange(stages, dtype=jnp.int32)
    counts = jnp.sum((stage[None, :] == numbers[:, None]).astype(jnp.int32), axis=1)
    begins = jnp.sum((stage[None, :] < numbers[:, None]).astype(jnp.int32), axis=1)
    return listing, jnp.stack([begins, counts], axis=1)


def body(leaf_density, m2m, v_source, v_class):
    axes = ("row", "col")
    size = m2m.shape[1]
    box_count = v_source.shape[0]
    rhs = leaf_density.shape[1] // (8 * box_count)
    device, ndev = lax.axis_index(axes), lax.axis_size(axes)

    ids = v_source.reshape(-1)
    owner = ids // box_count
    named = ids[:, None] == jnp.arange(ndev * box_count, dtype=jnp.int32)[None, :]
    needed = jnp.any(named, axis=0).reshape(ndev, box_count)
    local = jnp.arange(box_count, dtype=jnp.int32)
    earlier = (local[None, :] < local[:, None])[None]
    rank = jnp.sum((needed[:, None, :] & earlier).astype(jnp.int32), axis=2)
    slots = jnp.arange(LANES, dtype=jnp.int32)
    hit = needed[:, None, :] & (rank[:, None, :] == slots[None, :, None])
    wanted = jnp.sum(jnp.where(hit, local[None, None, :], 0), axis=2)

    def exchange(value):
        return lax.all_to_all(value, axes, split_axis=0, concat_axis=0, tiled=True)

    requested = exchange(wanted)
    pool, mh, ml = upward(leaf_density, m2m, box_count // 2)
    chosen = choose(pool, requested, 0, None)
    received = exchange(chosen)

    pair_rank = jnp.sum(jnp.where(named, rank.reshape(-1)[None, :], 0), axis=1)
    mine = owner == device
    source = jnp.where(mine, ids % box_count, owner)
    target = jnp.repeat(jnp.arange(box_count, dtype=jnp.int32), v_source.shape[1])
    codes = v_class.reshape(-1) * 4096 + target * 256 + source
    listing, spans = stage_lists(jnp.where(mine, 0, 1 + pair_rank), codes, 1 + CAP)

    first = (device * (box_count // 8)) % 8
    current = coarse_partial(pool, mh, ml, tie(first.reshape(1).astype(jnp.int32), chosen), rhs)
    group_size = 64 // box_count
    for bit in range(group_size.bit_length() - 1):
        pairs = [(i, i ^ (1 << bit)) for i in range(ndev)]
        current = current + lax.ppermute(current, axes, pairs)
    share = rhs // group_size
    coarse = lax.dynamic_slice_in_dim(current, (device % group_size) * share, share, 1)

    chosen_second = choose(pool, requested, 1, chosen)
    there = jnp.sum(needed.astype(jnp.int32), axis=1)
    every = jnp.ones((box_count // 2,), jnp.int32)
    acc = field(pool, None, listing, spans[0], every, box_count, size, False, chosen_second)
    received_second = exchange(tie(chosen_second, (acc, coarse)))
    acc = field(received, acc, listing, spans[1], there, box_count, size, False, None)
    out = field(received_second, acc, listing, spans[2], there - 1, box_count, size, True, None)
    return (coarse, out)


def solution(mesh):
    both = ("row", "col")
    return jax.shard_map(
        body,
        mesh=mesh,
        in_specs=(P(None, both), P(), P(both, None), P(both, None)),
        out_specs=(P(None, both), P(None, both)),
        check_vma=False,
    )
```
